128 devices in a mesh: cam: 32 (over x, z_lo, y), band: 4 (over z_hi, core).
Axes of the slice: x: 4, y: 4, z: 4 (z_hi: 2, z_lo: 2; z = z_hi * 2 + z_lo), core: 2. Of those that a mesh axis runs over, the one named last changes fastest.
Arguments:
- images: bfloat16 [32, 128, 64, 512], P('cam', None, 'band'), may hold values from -6 to 6
- weight: bfloat16 [3, 3, 256, 128], replicated, may hold values from -0.1875 to 0.1875
- offsets: int32 [32], replicated, may hold values from 0 to 127
- cotangent: bfloat16 [32, 64, 512, 128], P('cam', 'band'), may hold values from -6 to 6
Outputs:
- image_grad: float32 [32, 128, 64, 512], P('cam', None, 'band')
- weight_grad: float32 [3, 3, 256, 128], replicated
The draws below stay inside these ranges and needn't reach their ends.
All inputs are finite; a program needn't handle non-finite values.
Results may differ from the reference program's by a relative error of at most 0.0085.
Values may be sent and summed in bfloat16 or wider, within the bound.
No kernel may reach another device: no remote copies, remote signals or barrier semaphores. Data moves between devices by JAX's collectives and lax.ppermute only.
A program may use at most 192 MiB of HBM per device.

```python
import math
import jax
import jax.numpy as jnp
from jax import lax

C_IN = 128
C_OUT = 256
DISP = 128
W = 512
CAMS = 32
H = 64


def place_ends(result, stream_key, smallest, largest):
    spot = [jax.random.randint(jax.random.fold_in(stream_key, axis), (), 0, length) for axis, length in enumerate(result.shape)]
    main_axis = result.shape.index(max(result.shape))
    beside = spot[:main_axis] + [(spot[main_axis] + 1) % result.shape[main_axis]] + spot[main_axis + 1:]
    return result.at[tuple(spot)].set(smallest).at[tuple(beside)].set(largest)


def block_scale(stream_key, dims, shards, low, top_value):
    def one(dim, shards_of):
        heights = jax.random.uniform(jax.random.fold_in(jax.random.fold_in(stream_key, 6), dim), (shards_of,), jnp.float32, low / len(shards), top_value / len(shards))
        return jnp.repeat(jnp.exp(heights), dims[dim] // shards_of).reshape((-1,) + (1,) * (len(dims) - dim - 1))

    gain = one(*shards[0])
    for cut in shards[1:]:
        gain = gain * one(*cut)
    return gain


def noise(own_key, dims, width, most, shards=(), kind=jnp.bfloat16):
    result = width * jax.random.normal(own_key, dims, jnp.float32)
    if shards:
        result = result * block_scale(own_key, dims, shards, -0.22, 0.18)
    return jnp.clip(result, -most, most).astype(kind)


def setup_inputs(seed: int = 0) -> dict:
    arg_keys = jax.random.split(jax.random.key(seed), 5)
    images = noise(arg_keys[0], (CAMS, C_IN, H, W), 1.0, 6.0, ((0, 32), (2, 4)))
    weight = noise(arg_keys[1], (3, 3, C_OUT, C_IN), (9 * C_IN) ** -0.5, 0.1875)
    offsets = place_ends(jax.random.randint(arg_keys[2], (CAMS,), 0, W // 4), jax.random.fold_in(arg_keys[2], 1), 0, (W // 4) - 1).astype(jnp.int32)
    cotangent = noise(arg_keys[3], (CAMS, H, W, DISP), 1.0, 6.0, ((0, 32), (1, 4)))
    return {"images": images, "weight": weight, "offsets": offsets, "cotangent": cotangent}


def conv_rows(haloed, weight):
    row_count = haloed.shape[1] - 2
    columns = haloed.shape[2]
    padded = jnp.pad(haloed.astype(jnp.float32), ((0, 0), (0, 0), (1, 1)))
    summed = jnp.zeros((weight.shape[2], row_count, columns), jnp.float32)
    for tap_down in range(3):
        for tap_across in range(3):
            summed = summed + jnp.einsum('ka,ahw->khw', weight[tap_down, tap_across].astype(jnp.float32), padded[:, tap_down:tap_down + row_count, tap_across:tap_across + columns])
    return summed

def conv_back(haloed, weight):
    row_count = haloed.shape[1] - 2
    columns = haloed.shape[2]
    padded = jnp.pad(haloed.astype(jnp.float32), ((0, 0), (0, 0), (1, 1)))
    summed = jnp.zeros((weight.shape[3], row_count, columns), jnp.float32)
    for tap_down in range(3):
        for tap_across in range(3):
            summed = summed + jnp.einsum('ka,khw->ahw', weight[tap_down, tap_across].astype(jnp.float32), padded[:, 2 - tap_down:2 - tap_down + row_count, 2 - tap_across:2 - tap_across + columns])
    return summed

def local_weight(haloed, feat_grad):
    row_count = haloed.shape[1] - 2
    columns = haloed.shape[2]
    padded = jnp.pad(haloed.astype(jnp.float32), ((0, 0), (0, 0), (1, 1)))
    grads = feat_grad.astype(jnp.float32)
    return jnp.stack([jnp.stack([jnp.einsum('khw,ahw->ka', grads, padded[:, tap_down:tap_down + row_count, tap_across:tap_across + columns]) for tap_across in range(3)]) for tap_down in range(3)])

def key_windows(partner, offset, block_size):
    channels, row_count, columns = partner.shape
    padded = jnp.pad(partner, ((0, 0), (0, 0), (columns, block_size)))
    start = (columns - block_size + 1 - offset).astype(jnp.int32)
    keyed = lax.dynamic_slice_in_dim(padded, start, columns + block_size, 2)
    blocks = keyed.reshape(channels, row_count, columns // block_size + 1, block_size)
    return jnp.concatenate([blocks[:, :, :-1], blocks[:, :, 1:]], axis=3)

def skew_take(products):
    row_count, count_blocks, block_size, twice = products.shape
    flat_scores = products.reshape(row_count, count_blocks, block_size * twice)
    flat_scores = jnp.pad(flat_scores, ((0, 0), (0, 0), (0, block_size)))
    diagonal = flat_scores.reshape(row_count, count_blocks, block_size, twice + 1)[..., :block_size]
    return jnp.flip(diagonal, axis=3).reshape(row_count, count_blocks * block_size, block_size)

def skew_place(grads):
    row_count, columns, block_size = grads.shape
    count_blocks = columns // block_size
    diagonal = jnp.flip(grads, axis=2).reshape(row_count, count_blocks, block_size, block_size)
    widened = jnp.pad(diagonal, ((0, 0), (0, 0), (0, 0), (0, block_size + 1)))
    flat_grads = widened.reshape(row_count, count_blocks, block_size * (2 * block_size + 1))
    return flat_grads[..., :2 * block_size * block_size].reshape(row_count, count_blocks, block_size, 2 * block_size)

def score_grad(query_feats, partner, offset, cotangent):
    channels, row_count, columns = query_feats.shape
    block_size = cotangent.shape[2]
    windows = key_windows(partner, offset, block_size).astype(jnp.float32)
    queries = query_feats.reshape(channels, row_count, columns // block_size, block_size).astype(jnp.float32)
    products = jnp.einsum('krbi,krbj->rbij', queries, windows)
    scale = 1.0 / math.sqrt(channels)
    squashed = jnp.tanh(skew_take(products) * scale)
    return (cotangent.astype(jnp.float32) * (1.0 - squashed * squashed) * scale).astype(jnp.bfloat16)

def query_grad(sgrad, partner, offset):
    block_size = sgrad.shape[2]
    windows = key_windows(partner, offset, block_size).astype(jnp.float32)
    placed = skew_place(sgrad).astype(jnp.float32)
    return jnp.einsum('rbij,krbj->krbi', placed, windows).reshape(partner.shape)

def key_grad(sgrad, query_feats, offset):
    channels, row_count, columns = query_feats.shape
    block_size = sgrad.shape[2]
    placed = skew_place(sgrad).astype(jnp.float32)
    queries = query_feats.reshape(channels, row_count, columns // block_size, block_size).astype(jnp.float32)
    window_grad = jnp.einsum('rbij,krbi->krbj', placed, queries)
    head_part = jnp.pad(window_grad[..., :block_size], ((0, 0), (0, 0), (0, 1), (0, 0)))
    tail_part = jnp.pad(window_grad[..., block_size:], ((0, 0), (0, 0), (1, 0), (0, 0)))
    keyed = (head_part + tail_part).reshape(channels, row_count, columns + block_size)
    padded = jnp.pad(keyed, ((0, 0), (0, 0), (0, columns)))
    start = (offset + block_size - 1).astype(jnp.int32)
    return lax.dynamic_slice_in_dim(padded, start, columns, 2).astype(jnp.bfloat16)

def pad_rows(block):
    return jnp.pad(block, ((0, 0), (1, 1), (0, 0)))

def reference(images, weight, offsets, cotangent):
    feats = lax.map(lambda camera_image: conv_rows(pad_rows(camera_image), weight).astype(jnp.bfloat16), images)
    cameras = jnp.arange(CAMS, dtype=jnp.int32)
    partner_index = ((cameras + 1) % CAMS).astype(jnp.int32)

    def per_camera(camera):
        query_feats = feats[camera]
        partner = feats[partner_index[camera]]
        offset = offsets[camera]
        sgrad = score_grad(query_feats, partner, offset, cotangent[camera])
        return (query_grad(sgrad, partner, offset), key_grad(sgrad, query_feats, offset))
    query_grads, key_grads = lax.map(per_camera, cameras)
    from_lower = jnp.roll(key_grads, 1, axis=0).astype(jnp.float32)
    feat_grad = (query_grads + from_lower).astype(jnp.bfloat16)
    image_grad = lax.map(lambda grads: conv_back(pad_rows(grads), weight), feat_grad)

    def add_camera(summed, pair):
        camera_image, grads = pair
        return (summed + local_weight(pad_rows(camera_image), grads), None)
    start_sum = jnp.zeros((3, 3, C_OUT, C_IN), jnp.float32)
    total_grad, unused = lax.scan(add_camera, start_sum, (images, feat_grad))
    weight_grad = total_grad * (1.0 / math.sqrt(CAMS * H * W))
    return (image_grad, weight_grad)
```

```python
import math

import jax
import jax.numpy as jnp
from jax import lax
from jax.experimental import pallas as pl
from jax.experimental.pallas import tpu as pltpu
from jax.sharding import PartitionSpec as P

C_IN = 128
C_OUT = 256
DISP = 128
F32 = jnp.float32
BF16 = jnp.bfloat16
MIB = 1024 * 1024


def params(limit_mib):
    return pltpu.CompilerParams(
        dimension_semantics=("arbitrary",), vmem_limit_bytes=limit_mib * MIB
    )


def without_lane(tile, place):
    lane = lax.broadcasted_iota(jnp.int32, tile.shape, 1)
    return jnp.where(lane == place, 0.0, tile)


def shifted_right(x):
    moved = pltpu.roll(x, 1, 1)
    return jnp.concatenate([without_lane(moved[:, :DISP], 0), moved[:, DISP:]], axis=1)


def shifted_left(x):
    width = x.shape[1]
    moved = pltpu.roll(x, width - 1, 1)
    return jnp.concatenate(
        [moved[:, : width - DISP], without_lane(moved[:, width - DISP :], DISP - 1)], axis=1
    )


def put_taps(taps_ref, place, row):
    wide = row.astype(F32)
    taps_ref[place, :C_IN, :] = shifted_right(wide).astype(BF16)
    taps_ref[place, C_IN : 2 * C_IN, :] = row
    taps_ref[place, 2 * C_IN :, :] = shifted_left(wide).astype(BF16)


def next_row(taps_ref, x_ref, r):
    @pl.when(r == 0)
    def _():
        put_taps(taps_ref, 1, x_ref[0])
        put_taps(taps_ref, 2, x_ref[1])

    taps_ref[0] = taps_ref[1]
    taps_ref[1] = taps_ref[2]
    put_taps(taps_ref, 2, x_ref[r + 2])


def conv_row(weight_ref, taps_ref):
    patch = taps_ref[...].reshape(9 * C_IN, taps_ref.shape[2])
    return jnp.dot(weight_ref[...], patch, preferred_element_type=F32)


def own_kernel(x_ref, weight_ref, cot_ref, feat_ref, featt_ref, skew_ref, tap_ref, taps):
    r = pl.program_id(0)

    next_row(taps, x_ref, r)
    feat = conv_row(weight_ref, taps)
    feat_ref[0] = feat.astype(BF16)
    featt_ref[0] = feat.T.astype(BF16)
    tap_ref[0] = taps[1]
    rows = lax.broadcasted_iota(jnp.int32, (DISP, DISP), 0)
    cols = lax.broadcasted_iota(jnp.int32, (DISP, DISP), 1)
    exchange = jnp.where(rows + cols == DISP - 1, 1.0, 0.0).astype(BF16)
    flipped = jnp.dot(cot_ref[0], exchange, preferred_element_type=F32)
    blocks = flipped.shape[0] // DISP
    for b in range(blocks):
        part = flipped[b * DISP : (b + 1) * DISP]
        wide = jnp.concatenate([part, jnp.zeros_like(part)], axis=1)
        skew_ref[0, b * DISP : (b + 1) * DISP] = pltpu.roll(
            wide, 0, 1, stride=1, stride_axis=0
        ).astype(BF16)


def own_side(x_haloed, weight_fwd, cot_haloed):
    rows, columns, _ = cot_haloed.shape
    row = lambda *tail: pl.BlockSpec((1,) + tail, lambda r: (r,) + (0,) * len(tail))
    return pl.pallas_call(
        own_kernel,
        grid=(rows,),
        in_specs=[
            pl.BlockSpec(x_haloed.shape, lambda r: (0, 0, 0), pipeline_mode=pl.Buffered(1)),
            pl.BlockSpec(weight_fwd.shape, lambda r: (0, 0), pipeline_mode=pl.Buffered(1)),
            row(columns, DISP),
        ],
        out_specs=[
            row(C_OUT, columns),
            row(columns, C_OUT),
            row(columns, 2 * DISP),
            row(3 * C_IN, columns),
        ],
        out_shape=[
            jax.ShapeDtypeStruct((rows, C_OUT, columns), BF16),
            jax.ShapeDtypeStruct((rows, columns, C_OUT), BF16),
            jax.ShapeDtypeStruct((rows, columns, 2 * DISP), BF16),
            jax.ShapeDtypeStruct((rows, 3 * C_IN, columns), BF16),
        ],
        scratch_shapes=[pltpu.VMEM((3, 3 * C_IN, columns), BF16)],
        compiler_params=params(40),
        name="own_side",
    )(x_haloed, weight_fwd, cot_haloed)


def pair_kernel(
    off_ref, x_ref, weight_ref, feat_ref, featt_ref, skew_ref, *rest
):
    query_ref, key_ref, tap_ref, taps = rest[-4:]
    r = pl.program_id(0)

    next_row(taps, x_ref, r)
    tap_ref[0] = taps[1]
    feat = conv_row(weight_ref, taps).astype(BF16).astype(F32)
    columns = feat.shape[1]
    blocks = columns // DISP
    wide = columns + 2 * DISP
    move = off_ref[0] + (DISP - 1)
    padded = jnp.concatenate([feat, jnp.zeros((C_OUT, 2 * DISP), F32)], axis=1)
    keyed = pltpu.roll(padded, move, 1)[:, : columns + DISP].astype(BF16)
    scale = 1.0 / math.sqrt(C_OUT)
    heads, tails = [], []
    for b in range(blocks):
        here = slice(b * DISP, (b + 1) * DISP)
        window = keyed[:, b * DISP : (b + 2) * DISP]
        products = jnp.dot(featt_ref[0, here, :], window, preferred_element_type=F32)
        squashed = jnp.tanh(products * scale)
        placed = (
            skew_ref[0, here, :].astype(F32) * (1.0 - squashed * squashed) * scale
        ).astype(BF16)
        query_ref[0, :, here] = lax.dot_general(
            window, placed, (((1,), (1,)), ((), ())), preferred_element_type=F32
        ).astype(BF16)
        grad = jnp.dot(feat_ref[0, :, here], placed, preferred_element_type=F32)
        heads.append(grad[:, :DISP])
        tails.append(grad[:, DISP:])
    tiles = [heads[0]]
    for b in range(1, blocks):
        tiles.append(heads[b] + tails[b - 1])
    tiles += [tails[-1], jnp.zeros_like(tails[-1])]
    key_ref[0] = pltpu.roll(jnp.concatenate(tiles, axis=1), wide - move, 1)[:, :columns].astype(
        BF16
    )


def pair_side(offset, x_part, weight_fwd, feat, featt, skew, base, carried):
    rows, _, columns = feat.shape
    count = x_part.shape[0] - 2
    row = lambda *tail: pl.BlockSpec((1,) + tail, lambda r, off: (r + base,) + (0,) * len(tail))
    whole = lambda a: pl.BlockSpec(
        a.shape, lambda r, off: (0,) * a.ndim, pipeline_mode=pl.Buffered(1)
    )
    operands = [x_part, weight_fwd, feat, featt, skew]
    in_specs = [
        whole(x_part),
        whole(weight_fwd),
        row(C_OUT, columns),
        row(columns, C_OUT),
        row(columns, 2 * DISP),
    ]
    aliases = {}
    if carried is not None:
        for i, buffer in enumerate(carried):
            aliases[1 + len(operands)] = i
            operands.append(buffer)
            in_specs.append(pl.BlockSpec(memory_space=pl.ANY))
    return pl.pallas_call(
        pair_kernel,
        grid_spec=pltpu.PrefetchScalarGridSpec(
            num_scalar_prefetch=1,
            grid=(count,),
            in_specs=in_specs,
            out_specs=[row(C_OUT, columns), row(C_OUT, columns), row(3 * C_IN, columns)],
            scratch_shapes=[pltpu.VMEM((3, 3 * C_IN, columns), BF16)],
        ),
        out_shape=[
            jax.ShapeDtypeStruct((rows, C_OUT, columns), BF16),
            jax.ShapeDtypeStruct((rows, C_OUT, columns), BF16),
            jax.ShapeDtypeStruct((rows, 3 * C_IN, columns), BF16),
        ],
        input_output_aliases=aliases,
        compiler_params=params(32),
        name="pair_side",
    )(offset, *operands)


def back_row(weight_ref, grad_ref, r):
    columns = grad_ref.shape[2]
    patch = grad_ref[pl.ds(r, 3)].reshape(3 * C_OUT, columns)
    taps = jnp.dot(weight_ref[...], patch, preferred_element_type=F32)
    return (
        taps[C_IN : 2 * C_IN]
        + shifted_left(taps[:C_IN])
        + shifted_right(taps[2 * C_IN :])
    )


def key_back_kernel(grad_ref, weight_ref, out_ref):
    out_ref[0] = back_row(weight_ref, grad_ref, pl.program_id(0)).astype(BF16)


def key_back(key, weight_bwd):
    rows, _, columns = key.shape
    return pl.pallas_call(
        key_back_kernel,
        grid=(rows - 2,),
        in_specs=[
            pl.BlockSpec(key.shape, lambda r: (0, 0, 0), pipeline_mode=pl.Buffered(1)),
            pl.BlockSpec(weight_bwd.shape, lambda r: (0, 0), pipeline_mode=pl.Buffered(1)),
        ],
        out_specs=pl.BlockSpec((1, C_IN, columns), lambda r: (r, 0, 0)),
        out_shape=jax.ShapeDtypeStruct((rows - 2, C_IN, columns), BF16),
        compiler_params=params(24),
        name="key_back",
    )(key, weight_bwd)


def image_back_kernel(grad_ref, weight_ref, recv_ref, out_ref):
    out_ref[0] = back_row(weight_ref, grad_ref, pl.program_id(0)) + recv_ref[0].astype(F32)


def image_back(query, weight_bwd, received):
    rows, _, columns = query.shape
    count = rows - 2
    out = pl.pallas_call(
        image_back_kernel,
        grid=(count,),
        in_specs=[
            pl.BlockSpec(query.shape, lambda r: (0, 0, 0), pipeline_mode=pl.Buffered(1)),
            pl.BlockSpec(weight_bwd.shape, lambda r: (0, 0), pipeline_mode=pl.Buffered(1)),
            pl.BlockSpec((1, C_IN, columns), lambda r: (r, 0, 0)),
        ],
        out_specs=pl.BlockSpec((1, C_IN, columns), lambda r: (r, 0, 0)),
        out_shape=jax.ShapeDtypeStruct((count, C_IN, columns), F32),
        compiler_params=params(32),
        name="image_back",
    )(query, weight_bwd, received)
    return jnp.transpose(out, (1, 0, 2))


def weight_kernel(query_ref, key_ref, own_ref, partner_ref, out_ref, acc):
    r = pl.program_id(0)
    columns = query_ref.shape[2]
    contract = (((1,), (1,)), ((), ()))
    own = own_ref[pl.ds(r, 3)].reshape(9 * C_IN, columns)
    partner = partner_ref[pl.ds(r, 3)].reshape(9 * C_IN, columns)
    term = lax.dot_general(
        query_ref[0], own, contract, preferred_element_type=F32
    ) + lax.dot_general(key_ref[0], partner, contract, preferred_element_type=F32)

    @pl.when(r == 0)
    def _():
        acc[...] = term

    @pl.when(r > 0)
    def _():
        acc[...] += term

    @pl.when(r == pl.num_programs(0) - 1)
    def _():
        for tap in range(9):
            out_ref[tap] = acc[:, tap * C_IN : (tap + 1) * C_IN].astype(BF16)


def weight_term(query, key, own_taps, partner_taps):
    rows, _, columns = query.shape
    inner = pl.BlockSpec((1, C_OUT, columns), lambda r: (r + 1, 0, 0))
    taps = pl.BlockSpec(own_taps.shape, lambda r: (0, 0, 0), pipeline_mode=pl.Buffered(1))
    return pl.pallas_call(
        weight_kernel,
        grid=(rows - 2,),
        in_specs=[inner, inner, taps, taps],
        out_specs=pl.BlockSpec((9, C_OUT, C_IN), lambda r: (0, 0, 0)),
        out_shape=jax.ShapeDtypeStruct((9, C_OUT, C_IN), BF16),
        scratch_shapes=[pltpu.VMEM((C_OUT, 9 * C_IN), F32)],
        compiler_params=params(40),
        name="weight_term",
    )(query, key, own_taps, partner_taps)


def passed_along(x, axis, by):
    size = lax.axis_size(axis)
    return lax.ppermute(x, axis, [(i, (i + by) % size) for i in range(size)])


def shifted_bands(x, by):
    size = lax.axis_size("band")
    return lax.ppermute(
        x, "band", [(i, i + by) for i in range(size) if 0 <= i + by < size]
    )


def lookup(table, position):
    places = jnp.arange(table.shape[0], dtype=jnp.int32)
    return jnp.sum(jnp.where(places == position, table, 0), dtype=jnp.int32)


def summed_everywhere(term):
    axes = ("cam", "band")
    count = lax.axis_size("cam") * lax.axis_size("band")
    pieces = term.reshape(count, -1, C_IN)
    mine = lax.all_to_all(pieces, axes, split_axis=0, concat_axis=0, tiled=True)
    piece = jnp.sum(mine.astype(F32), axis=0, keepdims=True).astype(BF16)
    spread = jnp.broadcast_to(piece, pieces.shape)
    return lax.all_to_all(spread, axes, split_axis=0, concat_axis=0, tiled=True)


def per_device(images, weight, offsets, cotangent):
    image = jnp.transpose(images[0], (1, 0, 2))
    cot = cotangent[0]
    rows = image.shape[0]
    columns = image.shape[2]
    part = (rows - 4) // 2
    edges = jnp.concatenate([image[:2], image[-2:]], axis=0)
    partner_edges = passed_along(edges, "cam", -1)
    upper = jnp.concatenate([image[-2:], cot[-1].T[None]], axis=0)
    lower = jnp.concatenate([image[:2], cot[0].T[None]], axis=0)
    low = shifted_bands(upper, 1)
    high = shifted_bands(lower, -1)
    first = passed_along(image[2 : 2 + part], "cam", -1)
    second = passed_along(image[2 + part : 2 + 2 * part], "cam", -1)
    partner_low = shifted_bands(partner_edges[2:], 1)
    partner_high = shifted_bands(partner_edges[:2], -1)

    offset = lookup(offsets, lax.axis_index("cam")).reshape(1)
    weight_fwd = jnp.transpose(weight, (2, 0, 1, 3)).reshape(C_OUT, 9 * C_IN)
    weight_bwd = jnp.transpose(weight[::-1], (1, 3, 0, 2)).reshape(3 * C_IN, 3 * C_OUT)

    haloed = jnp.concatenate([low[:2], image, high[:2]], axis=0)
    cot_haloed = jnp.concatenate([low[2].T[None], cot, high[2].T[None]], axis=0)
    feat, featt, skew, own_taps = own_side(haloed, weight_fwd, cot_haloed)

    top = jnp.concatenate([partner_low, partner_edges[:2], first], axis=0)
    bottom = jnp.concatenate([first[-2:], second, partner_edges[2:], partner_high], axis=0)
    carried = pair_side(offset, top, weight_fwd, feat, featt, skew, 0, None)
    query, key, partner_taps = pair_side(
        offset, bottom, weight_fwd, feat, featt, skew, top.shape[0] - 2, carried
    )
    received = passed_along(key_back(key, weight_bwd), "cam", 1)
    term = weight_term(query, key, own_taps, partner_taps)
    total = summed_everywhere(term)
    normalizer = 1.0 / math.sqrt(lax.axis_size("cam") * lax.axis_size("band") * rows * columns)
    weight_grad = total.astype(F32).reshape(weight.shape) * normalizer
    image_grad = image_back(query, weight_bwd, received)
    return (image_grad[None], weight_grad)


def solution(mesh):
    in_specs = (P("cam", None, "band", None), P(), P(), P("cam", "band", None, None))
    out_specs = (P("cam", None, "band", None), P())
    return jax.shard_map(
        per_device, mesh=mesh, in_specs=in_specs, out_specs=out_specs, check_vma=False
    )
```

```python
import math

import jax
import jax.numpy as jnp
from jax import lax
from jax.experimental import pallas as pl
from jax.experimental.pallas import tpu as pltpu
from jax.sharding import PartitionSpec as P

C_IN = 128
C_OUT = 256
DISP = 128
F32 = jnp.float32
BF16 = jnp.bfloat16
MIB = 1024 * 1024


def params(limit_mib=60):
    return pltpu.CompilerParams(
        dimension_semantics=("arbitrary",), vmem_limit_bytes=limit_mib * MIB
    )


def without_lane(tile, place):
    lane = lax.broadcasted_iota(jnp.int32, tile.shape, 1)
    return jnp.where(lane == place, 0.0, tile)


def shifted_right(x):
    moved = pltpu.roll(x, 1, 1)
    return jnp.concatenate([without_lane(moved[:, :DISP], 0), moved[:, DISP:]], axis=1)


def shifted_left(x):
    width = x.shape[1]
    moved = pltpu.roll(x, width - 1, 1)
    return jnp.concatenate(
        [moved[:, : width - DISP], without_lane(moved[:, width - DISP :], DISP - 1)], axis=1
    )


def put_taps(taps_ref, place, row):
    wide = row.astype(F32)
    taps_ref[place, :C_IN, :] = shifted_right(wide).astype(BF16)
    taps_ref[place, C_IN : 2 * C_IN, :] = row
    taps_ref[place, 2 * C_IN :, :] = shifted_left(wide).astype(BF16)


def row_at(pieces, refs, t):
    for (start, count), ref in zip(pieces, refs):
        if t < count:
            return ref[start + t]
        t -= count


def fetch_row(pieces, refs, row_ref, t):
    first = 0
    for (start, count), ref in zip(pieces, refs):
        low, high = first, first + count

        @pl.when((t >= low) & (t < high))
        def _(ref=ref, start=start, low=low):
            row_ref[...] = ref[t - low + start]

        first = high


def next_row(pieces, refs, taps_ref, row_ref, r):
    total = sum(count for _, count in pieces)

    @pl.when(r == 0)
    def _():
        put_taps(taps_ref, 1, row_at(pieces, refs, 0))
        put_taps(taps_ref, 2, row_at(pieces, refs, 1))

    fetch_row(pieces, refs, row_ref, jnp.minimum(r + 2, total - 1))
    taps_ref[0] = taps_ref[1]
    taps_ref[1] = taps_ref[2]
    put_taps(taps_ref, 2, row_ref[...])


def conv_row(weight_ref, taps_ref):
    patch = taps_ref[...].reshape(9 * C_IN, taps_ref.shape[2])
    return jnp.dot(weight_ref[...], patch, preferred_element_type=F32)


def whole(a):
    return pl.BlockSpec(a.shape, lambda *_: (0,) * a.ndim, pipeline_mode=pl.Buffered(1))


def own_kernel(pieces, carried, *refs):
    count = len(pieces)
    x_refs = refs[:count]
    weight_ref, cot_ref = refs[count : count + 2]
    feat_ref, featt_ref, skew_ref, tap_ref, taps, row = refs[count + 2 + carried :]
    r = pl.program_id(0)
    next_row(pieces, x_refs, taps, row, r)
    feat = conv_row(weight_ref, taps)
    feat_ref[0] = feat.astype(BF16)
    featt_ref[0] = feat.T.astype(BF16)
    tap_ref[0] = taps[1]
    rows = lax.broadcasted_iota(jnp.int32, (DISP, DISP), 0)
    cols = lax.broadcasted_iota(jnp.int32, (DISP, DISP), 1)
    exchange = jnp.where(rows + cols == DISP - 1, 1.0, 0.0).astype(BF16)
    flipped = jnp.dot(cot_ref[0], exchange, preferred_element_type=F32)
    blocks = flipped.shape[0] // DISP
    for b in range(blocks):
        part = flipped[b * DISP : (b + 1) * DISP]
        wide = jnp.concatenate([part, jnp.zeros_like(part)], axis=1)
        skew_ref[0, b * DISP : (b + 1) * DISP] = pltpu.roll(
            wide, 1, 1, stride=1, stride_axis=0
        ).astype(BF16)


def own_side(pieces, parts, weight_fwd, cot, rows, place, cot_place, carried):
    _, columns, _ = cot.shape
    count = sum(n for _, n in pieces) - 2
    row = lambda *tail: pl.BlockSpec((1,) + tail, lambda r: (place(r),) + (0,) * len(tail))
    operands = [*parts, weight_fwd, cot]
    in_specs = [
        *[whole(part) for part in parts],
        whole(weight_fwd),
        pl.BlockSpec((1, columns, DISP), lambda r: (cot_place(r), 0, 0)),
    ]
    aliases = {}
    for i, buffer in enumerate(carried):
        aliases[len(operands)] = i
        operands.append(buffer)
        in_specs.append(pl.BlockSpec(memory_space=pl.ANY))
    return pl.pallas_call(
        lambda *refs: own_kernel(pieces, len(carried), *refs),
        grid=(count,),
        in_specs=in_specs,
        out_specs=[
            row(C_OUT, columns),
            row(columns, C_OUT),
            row(columns, 2 * DISP),
            row(3 * C_IN, columns),
        ],
        out_shape=[
            jax.ShapeDtypeStruct((rows, C_OUT, columns), BF16),
            jax.ShapeDtypeStruct((rows, columns, C_OUT), BF16),
            jax.ShapeDtypeStruct((rows, columns, 2 * DISP), BF16),
            jax.ShapeDtypeStruct((rows, 3 * C_IN, columns), BF16),
        ],
        input_output_aliases=aliases,
        scratch_shapes=[
            pltpu.VMEM((3, 3 * C_IN, columns), BF16),
            pltpu.VMEM((C_IN, columns), BF16),
        ],
        compiler_params=params(),
        name="own_side",
    )(*operands)


def pair_kernel(pieces, carried, off_ref, *refs):
    count = len(pieces)
    x_refs = refs[:count]
    weight_ref, feat_ref, featt_ref, skew_ref = refs[count : count + 4]
    query_ref, key_ref, tap_ref, taps, row, keys = refs[count + 4 + carried :]
    r = pl.program_id(0)
    blocks = feat_ref.shape[2] // DISP
    columns = blocks * DISP
    offset = off_ref[0]
    scale = 1.0 / math.sqrt(C_OUT)
    keyed = keys[...]
    next_row(pieces, x_refs, taps, row, r)
    feat = conv_row(weight_ref, taps).astype(BF16).astype(F32)

    heads, tails = [], []
    for b in range(blocks):
        here = slice(b * DISP, (b + 1) * DISP)
        window = keyed[:, b * DISP : (b + 2) * DISP]
        products = jnp.dot(featt_ref[0, here, :], window, preferred_element_type=F32)
        squashed = jnp.tanh(products * scale)
        placed = (
            skew_ref[0, here, :].astype(F32) * (1.0 - squashed * squashed) * scale
        ).astype(BF16)
        query_ref[0, :, here] = lax.dot_general(
            window, placed, (((1,), (1,)), ((), ())), preferred_element_type=F32
        ).astype(BF16)
        grad = jnp.dot(feat_ref[0, :, here], placed, preferred_element_type=F32)
        heads.append(grad[:, :DISP])
        tails.append(grad[:, DISP:])
    back = jnp.where(offset == 0, 0, DISP - offset)
    lane = lax.broadcasted_iota(jnp.int32, (C_OUT, DISP), 1)
    moved = []
    for b in range(blocks):
        tile = tails[b] if b == blocks - 1 else tails[b] + heads[b + 1]
        moved.append(pltpu.roll(tile, back, 1))
    moved.append(jnp.zeros_like(moved[0]))
    for b in range(blocks):
        key_ref[0, :, b * DISP : (b + 1) * DISP] = jnp.where(
            lane < DISP - offset, moved[b], moved[b + 1]
        ).astype(BF16)
    tap_ref[0] = taps[0]

    empty = jnp.zeros((C_OUT, DISP), F32)
    moved = [empty]
    for b in range(blocks):
        moved.append(pltpu.roll(feat[:, b * DISP : (b + 1) * DISP], offset, 1))
    keys[:, :DISP] = empty.astype(BF16)
    for b in range(blocks):
        keys[:, (b + 1) * DISP : (b + 2) * DISP] = jnp.where(
            lane >= offset, moved[b + 1], moved[b]
        ).astype(BF16)


def pair_side(offset, pieces, parts, weight_fwd, feat, featt, skew, place, carried):
    rows, _, columns = feat.shape
    count = sum(n for _, n in pieces) - 2
    row = lambda *tail: pl.BlockSpec(
        (1,) + tail, lambda r, off: (place(jnp.maximum(r - 1, 0)),) + (0,) * len(tail)
    )
    operands = [*parts, weight_fwd, feat, featt, skew]
    in_specs = [
        *[whole(part) for part in parts],
        whole(weight_fwd),
        row(C_OUT, columns),
        row(columns, C_OUT),
        row(columns, 2 * DISP),
    ]
    aliases = {}
    for i, buffer in enumerate(carried):
        aliases[1 + len(operands)] = i
        operands.append(buffer)
        in_specs.append(pl.BlockSpec(memory_space=pl.ANY))
    return pl.pallas_call(
        lambda *refs: pair_kernel(pieces, len(carried), *refs),
        grid_spec=pltpu.PrefetchScalarGridSpec(
            num_scalar_prefetch=1,
            grid=(count + 1,),
            in_specs=in_specs,
            out_specs=[row(C_OUT, columns), row(C_OUT, columns), row(3 * C_IN, columns)],
            scratch_shapes=[
                pltpu.VMEM((3, 3 * C_IN, columns), BF16),
                pltpu.VMEM((C_IN, columns), BF16),
                pltpu.VMEM((C_OUT, columns + DISP), BF16),
            ],
        ),
        out_shape=[
            jax.ShapeDtypeStruct((rows, C_OUT, columns), BF16),
            jax.ShapeDtypeStruct((rows, C_OUT, columns), BF16),
            jax.ShapeDtypeStruct((rows, 3 * C_IN, columns), BF16),
        ],
        input_output_aliases=aliases,
        compiler_params=params(),
        name="pair_side",
    )(offset, *operands)


def back_row(weight_ref, grad_ref, r):
    taps = jnp.dot(weight_ref[:, 2 * C_OUT :], grad_ref[r], preferred_element_type=F32)
    taps += jnp.dot(
        weight_ref[:, C_OUT : 2 * C_OUT], grad_ref[r + 1], preferred_element_type=F32
    )
    taps += jnp.dot(weight_ref[:, :C_OUT], grad_ref[r + 2], preferred_element_type=F32)
    return (
        taps[C_IN : 2 * C_IN] + shifted_left(taps[:C_IN]) + shifted_right(taps[2 * C_IN :])
    )


GROUP = 4


def window(depth, columns, first=0, step=GROUP):
    return pl.BlockSpec(
        (pl.Element(GROUP + 2), pl.Element(depth), pl.Element(columns)),
        lambda s: (s * step + first, 0, 0),
    )


def key_back_kernel(grad_ref, weight_ref, out_ref):
    for r in range(GROUP):
        out_ref[r] = back_row(weight_ref, grad_ref, r).astype(BF16)


def key_back(key, weight_bwd, first, step, groups):
    columns = key.shape[2]
    return pl.pallas_call(
        key_back_kernel,
        grid=(groups,),
        in_specs=[window(C_OUT, columns, first, step), whole(weight_bwd)],
        out_specs=pl.BlockSpec((GROUP, C_IN, columns), lambda s: (s, 0, 0)),
        out_shape=jax.ShapeDtypeStruct((groups * GROUP, C_IN, columns), BF16),
        compiler_params=params(),
        name="key_back",
    )(key, weight_bwd)


def image_back_kernel(grad_ref, weight_ref, inner_ref, outer_ref, out_ref):
    s = pl.program_id(0)
    inside = (s > 0) & (s < pl.num_programs(0) - 1)
    for r in range(GROUP):
        out_ref[r] = back_row(weight_ref, grad_ref, r)

    @pl.when(inside)
    def _():
        out_ref[...] += inner_ref[...].astype(F32)

    @pl.when(jnp.logical_not(inside))
    def _():
        out_ref[...] += outer_ref[...].astype(F32)


def image_back(query, weight_bwd, inner, outer):
    rows, _, columns = query.shape
    count = rows - 2
    groups = count // GROUP
    block = (GROUP, C_IN, columns)
    out = pl.pallas_call(
        image_back_kernel,
        grid=(groups,),
        in_specs=[
            window(C_OUT, columns),
            whole(weight_bwd),
            pl.BlockSpec(block, lambda s: (jnp.clip(s - 1, 0, groups - 3), 0, 0)),
            pl.BlockSpec(block, lambda s: (s // (groups - 1), 0, 0)),
        ],
        out_specs=pl.BlockSpec(block, lambda s: (s, 0, 0)),
        out_shape=jax.ShapeDtypeStruct((count, C_IN, columns), F32),
        compiler_params=params(),
        name="image_back",
    )(query, weight_bwd, inner, outer)
    return jnp.transpose(out, (1, 0, 2))


def weight_kernel(query_ref, key_ref, own_ref, partner_ref, out_ref, acc):
    s = pl.program_id(0)
    columns = query_ref.shape[2]
    contract = (((1,), (1,)), ((), ()))

    @pl.when(s == 0)
    def _():
        acc[...] = jnp.zeros_like(acc)

    term = acc[...]
    for r in range(GROUP):
        own = own_ref[r : r + 3].reshape(9 * C_IN, columns)
        partner = partner_ref[r : r + 3].reshape(9 * C_IN, columns)
        term += lax.dot_general(query_ref[r + 1], own, contract, preferred_element_type=F32)
        term += lax.dot_general(key_ref[r + 1], partner, contract, preferred_element_type=F32)
    acc[...] = term

    @pl.when(s == pl.num_programs(0) - 1)
    def _():
        for tap in range(9):
            out_ref[tap] = acc[:, tap * C_IN : (tap + 1) * C_IN].astype(BF16)


def weight_term(query, key, own_taps, partner_taps):
    rows, _, columns = query.shape
    grads = window(C_OUT, columns)
    taps = window(3 * C_IN, columns)
    return pl.pallas_call(
        weight_kernel,
        grid=((rows - 2) // GROUP,),
        in_specs=[grads, grads, taps, taps],
        out_specs=pl.BlockSpec((9, C_OUT, C_IN), lambda s: (0, 0, 0)),
        out_shape=jax.ShapeDtypeStruct((9, C_OUT, C_IN), BF16),
        scratch_shapes=[pltpu.VMEM((C_OUT, 9 * C_IN), F32)],
        compiler_params=params(),
        name="weight_term",
    )(query, key, own_taps, partner_taps)


def passed_along(x, axis, by):
    size = lax.axis_size(axis)
    return lax.ppermute(x, axis, [(i, (i + by) % size) for i in range(size)])


def shifted_bands(x, by):
    size = lax.axis_size("band")
    return lax.ppermute(
        x, "band", [(i, i + by) for i in range(size) if 0 <= i + by < size]
    )


def diagonal(x, by):
    cams, bands = lax.axis_size("cam"), lax.axis_size("band")
    pairs = [
        ((c + 1) % cams * bands + b - by, c * bands + b)
        for c in range(cams)
        for b in range(bands)
        if 0 <= b - by < bands
    ]
    return lax.ppermute(x, ("cam", "band"), pairs)


def lookup(table, position):
    places = jnp.arange(table.shape[0], dtype=jnp.int32)
    return jnp.sum(jnp.where(places == position, table, 0), dtype=jnp.int32)


def summed_everywhere(term):
    axes = ("cam", "band")
    count = lax.axis_size("cam") * lax.axis_size("band")
    pieces = term.reshape(count, -1, C_IN)
    mine = lax.all_to_all(pieces, axes, split_axis=0, concat_axis=0, tiled=True)
    piece = jnp.sum(mine.astype(F32), axis=0, keepdims=True).astype(BF16)
    spread = jnp.broadcast_to(piece, pieces.shape)
    return lax.all_to_all(spread, axes, split_axis=0, concat_axis=0, tiled=True)


def per_device(images, weight, offsets, cotangent):
    image = jnp.transpose(images[0], (1, 0, 2))
    cot = cotangent[0]
    rows = image.shape[0]
    columns = image.shape[2]
    first, last = image[:2], image[-2:]
    low = shifted_bands(jnp.concatenate([last, cot[-1].T[None]], axis=0), 1)
    high = shifted_bands(jnp.concatenate([first, cot[0].T[None]], axis=0), -1)
    inner = passed_along(image[2:-2], "cam", -1)
    edges = passed_along(jnp.concatenate([first, last], axis=0), "cam", -1)
    partner_low = diagonal(last, 1)
    partner_high = diagonal(first, -1)

    offset = lookup(offsets, lax.axis_index("cam")).reshape(1)
    weight_fwd = jnp.transpose(weight, (2, 0, 1, 3)).reshape(C_OUT, 9 * C_IN)
    weight_bwd = jnp.transpose(weight, (1, 3, 0, 2)).reshape(3 * C_IN, 3 * C_OUT)

    total_rows = rows + 2
    own = own_side(
        ((0, rows),), (image,), weight_fwd, cot, total_rows, lambda r: r + 2, lambda r: r + 1, ()
    )
    carried = pair_side(
        offset, ((0, rows - 4),), (inner,), weight_fwd, *own[:3], lambda t: t + 4, ()
    )
    inner_back = key_back(carried[1], weight_bwd, GROUP, GROUP, rows // GROUP - 2)
    sent_inner = passed_along(inner_back, "cam", 1)
    own, carried, low, high = lax.optimization_barrier((own, carried, low, high))
    cot_ends = jnp.stack([low[2].T, cot[0], cot[-1], high[2].T])
    feat, featt, skew, own_taps = own_side(
        ((0, 2), (0, 2), (rows - 2, 2), (0, 2)),
        (low, image, image, high),
        weight_fwd,
        cot_ends,
        total_rows,
        lambda r: jnp.where(r < 2, r, jnp.maximum(r - 4, 0) + rows),
        lambda r: jnp.where(r < 2, r, jnp.maximum(r - 4, 0) + 2),
        own,
    )
    query, key, partner_taps = pair_side(
        offset,
        ((0, 2), (0, 2), (0, 2), (rows - 6, 2), (2, 2), (0, 2)),
        (partner_low, edges, inner, inner, edges, partner_high),
        weight_fwd,
        feat,
        featt,
        skew,
        lambda t: jnp.where(t < 4, t, jnp.maximum(t - 6, 0) + rows - 2),
        carried,
    )
    outer_back = key_back(key, weight_bwd, 0, rows - GROUP, 2)
    sent_outer = passed_along(outer_back, "cam", 1)
    key, sent_inner, _ = lax.optimization_barrier((key, sent_inner, outer_back))
    term = weight_term(query, key, own_taps, partner_taps)
    term, sent_outer = lax.optimization_barrier((term, sent_outer))
    total = summed_everywhere(term)
    normalizer = 1.0 / math.sqrt(lax.axis_size("cam") * lax.axis_size("band") * rows * columns)
    weight_grad = total.astype(F32).reshape(weight.shape) * normalizer
    query, total = lax.optimization_barrier((query, total))
    image_grad = image_back(query, weight_bwd, sent_inner, sent_outer)
    return (image_grad[None], weight_grad)


def solution(mesh):
    in_specs = (P("cam", None, "band", None), P(), P(), P("cam", "band", None, None))
    out_specs = (P("cam", None, "band", None), P())
    return jax.shard_map(
        per_device, mesh=mesh, in_specs=in_specs, out_specs=out_specs, check_vma=False
    )
```

```python
import math

import jax
import jax.numpy as jnp
from jax import lax
from jax.experimental import pallas as pl
from jax.experimental.pallas import tpu as pltpu
from jax.sharding import PartitionSpec as P

C_IN = 128
C_OUT = 256
DISP = 128
F32 = jnp.float32
BF16 = jnp.bfloat16
MIB = 1024 * 1024


def params(limit_mib=60):
    return pltpu.CompilerParams(
        dimension_semantics=("arbitrary",), vmem_limit_bytes=limit_mib * MIB
    )


def without_lane(tile, place):
    lane = lax.broadcasted_iota(jnp.int32, tile.shape, 1)
    return jnp.where(lane == place, 0.0, tile)


def shifted_right(x):
    moved = pltpu.roll(x, 1, 1)
    return jnp.concatenate([without_lane(moved[:, :DISP], 0), moved[:, DISP:]], axis=1)


def shifted_left(x):
    width = x.shape[1]
    moved = pltpu.roll(x, width - 1, 1)
    return jnp.concatenate(
        [moved[:, : width - DISP], without_lane(moved[:, width - DISP :], DISP - 1)], axis=1
    )


def put_taps(taps_ref, place, row):
    wide = row.astype(F32)
    taps_ref[place, :C_IN, :] = shifted_right(wide).astype(BF16)
    taps_ref[place, C_IN : 2 * C_IN, :] = row
    taps_ref[place, 2 * C_IN :, :] = shifted_left(wide).astype(BF16)


def row_at(pieces, refs, t):
    for (start, count), ref in zip(pieces, refs):
        if t < count:
            return ref[start + t]
        t -= count


def fetch_row(pieces, refs, row_ref, t):
    first = 0
    for (start, count), ref in zip(pieces, refs):
        low, high = first, first + count

        @pl.when((t >= low) & (t < high))
        def _(ref=ref, start=start, low=low):
            row_ref[...] = ref[t - low + start]

        first = high


def next_row(pieces, refs, taps_ref, row_ref, r):
    total = sum(count for _, count in pieces)

    @pl.when(r == 0)
    def _():
        put_taps(taps_ref, 1, row_at(pieces, refs, 0))
        put_taps(taps_ref, 2, row_at(pieces, refs, 1))

    fetch_row(pieces, refs, row_ref, jnp.minimum(r + 2, total - 1))
    taps_ref[0] = taps_ref[1]
    taps_ref[1] = taps_ref[2]
    put_taps(taps_ref, 2, row_ref[...])


def conv_row(weight_ref, taps_ref):
    patch = taps_ref[...].reshape(9 * C_IN, taps_ref.shape[2])
    return jnp.dot(weight_ref[...], patch, preferred_element_type=F32)


def whole(a):
    return pl.BlockSpec(a.shape, lambda *_: (0,) * a.ndim, pipeline_mode=pl.Buffered(1))


def own_kernel(pieces, carried, *refs):
    count = len(pieces)
    x_refs = refs[:count]
    weight_ref, cot_ref = refs[count : count + 2]
    feat_ref, featt_ref, skew_ref, tap_ref, taps, row = refs[count + 2 + carried :]
    r = pl.program_id(0)
    next_row(pieces, x_refs, taps, row, r)
    rows = lax.broadcasted_iota(jnp.int32, (DISP, DISP), 0)
    cols = lax.broadcasted_iota(jnp.int32, (DISP, DISP), 1)
    exchange = jnp.where(rows + cols == DISP - 1, 1.0, 0.0).astype(BF16)
    flipped = jnp.dot(cot_ref[0], exchange, preferred_element_type=F32)
    feat = conv_row(weight_ref, taps)
    blocks = flipped.shape[0] // DISP
    skewed = []
    for b in range(blocks):
        part = flipped[b * DISP : (b + 1) * DISP]
        wide = jnp.concatenate([part, jnp.zeros_like(part)], axis=1)
        skewed.append(pltpu.roll(wide, 1, 1, stride=1, stride_axis=0).astype(BF16))
    feat_ref[0] = feat.astype(BF16)
    featt_ref[0] = feat.T.astype(BF16)
    for b in range(blocks):
        skew_ref[0, b * DISP : (b + 1) * DISP] = skewed[b]
    tap_ref[0] = taps[1]


def own_side(pieces, parts, weight_fwd, cot, rows, place, cot_place, carried):
    _, columns, _ = cot.shape
    count = sum(n for _, n in pieces) - 2
    row = lambda *tail: pl.BlockSpec((1,) + tail, lambda r: (place(r),) + (0,) * len(tail))
    operands = [*parts, weight_fwd, cot]
    in_specs = [
        *[whole(part) for part in parts],
        whole(weight_fwd),
        pl.BlockSpec((1, columns, DISP), lambda r: (cot_place(r), 0, 0)),
    ]
    aliases = {}
    for i, buffer in enumerate(carried):
        aliases[len(operands)] = i
        operands.append(buffer)
        in_specs.append(pl.BlockSpec(memory_space=pl.ANY))
    return pl.pallas_call(
        lambda *refs: own_kernel(pieces, len(carried), *refs),
        grid=(count,),
        in_specs=in_specs,
        out_specs=[
            row(C_OUT, columns),
            row(columns, C_OUT),
            row(columns, 2 * DISP),
            row(3 * C_IN, columns),
        ],
        out_shape=[
            jax.ShapeDtypeStruct((rows, C_OUT, columns), BF16),
            jax.ShapeDtypeStruct((rows, columns, C_OUT), BF16),
            jax.ShapeDtypeStruct((rows, columns, 2 * DISP), BF16),
            jax.ShapeDtypeStruct((rows, 3 * C_IN, columns), BF16),
        ],
        input_output_aliases=aliases,
        scratch_shapes=[
            pltpu.VMEM((3, 3 * C_IN, columns), BF16),
            pltpu.VMEM((C_IN, columns), BF16),
        ],
        compiler_params=params(),
        name="own_side",
    )(*operands)


def pair_kernel(pieces, carried, off_ref, *refs):
    count = len(pieces)
    x_refs = refs[:count]
    weight_ref, feat_ref, featt_ref, skew_ref = refs[count : count + 4]
    query_ref, key_ref, tap_ref, taps, row, keys = refs[count + 4 + carried :]
    r = pl.program_id(0)
    blocks = feat_ref.shape[2] // DISP
    columns = blocks * DISP
    offset = off_ref[0]
    scale = 1.0 / math.sqrt(C_OUT)
    next_row(pieces, x_refs, taps, row, r)
    keyed = keys[...]
    windows = [keyed[:, b * DISP : (b + 2) * DISP] for b in range(blocks)]
    here = [slice(b * DISP, (b + 1) * DISP) for b in range(blocks)]
    products = [
        jnp.dot(featt_ref[0, here[b], :], windows[b], preferred_element_type=F32)
        for b in range(blocks)
    ]
    feat = conv_row(weight_ref, taps).astype(BF16).astype(F32)

    placed = []
    for b in range(blocks):
        squashed = jnp.tanh(products[b] * scale)
        placed.append(
            (skew_ref[0, here[b], :].astype(F32) * (1.0 - squashed * squashed) * scale).astype(
                BF16
            )
        )
    queries = [
        lax.dot_general(
            windows[b], placed[b], (((1,), (1,)), ((), ())), preferred_element_type=F32
        ).astype(BF16)
        for b in range(blocks)
    ]
    grads = [
        jnp.dot(feat_ref[0, :, here[b]], placed[b], preferred_element_type=F32)
        for b in range(blocks)
    ]
    heads = [grad[:, :DISP] for grad in grads]
    tails = [grad[:, DISP:] for grad in grads]
    back = jnp.where(offset == 0, 0, DISP - offset)
    lane = lax.broadcasted_iota(jnp.int32, (C_OUT, DISP), 1)
    moved = []
    for b in range(blocks):
        tile = tails[b] if b == blocks - 1 else tails[b] + heads[b + 1]
        moved.append(pltpu.roll(tile, back, 1))
    moved.append(jnp.zeros_like(moved[0]))
    shifted = [jnp.zeros((C_OUT, DISP), F32)]
    for b in range(blocks):
        shifted.append(pltpu.roll(feat[:, here[b]], offset, 1))
    for b in range(blocks):
        query_ref[0, :, here[b]] = queries[b]
        key_ref[0, :, here[b]] = jnp.where(
            lane < DISP - offset, moved[b], moved[b + 1]
        ).astype(BF16)
    tap_ref[0] = taps[0]
    keys[:, :DISP] = jnp.zeros((C_OUT, DISP), BF16)
    for b in range(blocks):
        keys[:, (b + 1) * DISP : (b + 2) * DISP] = jnp.where(
            lane >= offset, shifted[b + 1], shifted[b]
        ).astype(BF16)


def pair_side(offset, pieces, parts, weight_fwd, feat, featt, skew, place, carried):
    rows, _, columns = feat.shape
    count = sum(n for _, n in pieces) - 2
    row = lambda *tail: pl.BlockSpec(
        (1,) + tail, lambda r, off: (place(jnp.maximum(r - 1, 0)),) + (0,) * len(tail)
    )
    operands = [*parts, weight_fwd, feat, featt, skew]
    in_specs = [
        *[whole(part) for part in parts],
        whole(weight_fwd),
        row(C_OUT, columns),
        row(columns, C_OUT),
        row(columns, 2 * DISP),
    ]
    aliases = {}
    for i, buffer in enumerate(carried):
        aliases[1 + len(operands)] = i
        operands.append(buffer)
        in_specs.append(pl.BlockSpec(memory_space=pl.ANY))
    return pl.pallas_call(
        lambda *refs: pair_kernel(pieces, len(carried), *refs),
        grid_spec=pltpu.PrefetchScalarGridSpec(
            num_scalar_prefetch=1,
            grid=(count + 1,),
            in_specs=in_specs,
            out_specs=[row(C_OUT, columns), row(C_OUT, columns), row(3 * C_IN, columns)],
            scratch_shapes=[
                pltpu.VMEM((3, 3 * C_IN, columns), BF16),
                pltpu.VMEM((C_IN, columns), BF16),
                pltpu.VMEM((C_OUT, columns + DISP), BF16),
            ],
        ),
        out_shape=[
            jax.ShapeDtypeStruct((rows, C_OUT, columns), BF16),
            jax.ShapeDtypeStruct((rows, C_OUT, columns), BF16),
            jax.ShapeDtypeStruct((rows, 3 * C_IN, columns), BF16),
        ],
        input_output_aliases=aliases,
        compiler_params=params(),
        name="pair_side",
    )(offset, *operands)


def back_row(weight_ref, grad_ref, r):
    taps = jnp.dot(weight_ref[:, 2 * C_OUT :], grad_ref[r], preferred_element_type=F32)
    taps += jnp.dot(
        weight_ref[:, C_OUT : 2 * C_OUT], grad_ref[r + 1], preferred_element_type=F32
    )
    taps += jnp.dot(weight_ref[:, :C_OUT], grad_ref[r + 2], preferred_element_type=F32)
    return (
        taps[C_IN : 2 * C_IN] + shifted_left(taps[:C_IN]) + shifted_right(taps[2 * C_IN :])
    )


GROUP = 4


def window(depth, columns, first=0, step=GROUP):
    return pl.BlockSpec(
        (pl.Element(GROUP + 2), pl.Element(depth), pl.Element(columns)),
        lambda s: (s * step + first, 0, 0),
    )


def key_back_kernel(grad_ref, weight_ref, out_ref):
    for r in range(GROUP):
        out_ref[r] = back_row(weight_ref, grad_ref, r).astype(BF16)


def key_back(key, weight_bwd, first, step, groups):
    columns = key.shape[2]
    return pl.pallas_call(
        key_back_kernel,
        grid=(groups,),
        in_specs=[window(C_OUT, columns, first, step), whole(weight_bwd)],
        out_specs=pl.BlockSpec((GROUP, C_IN, columns), lambda s: (s, 0, 0)),
        out_shape=jax.ShapeDtypeStruct((groups * GROUP, C_IN, columns), BF16),
        compiler_params=params(),
        name="key_back",
    )(key, weight_bwd)


def image_back_kernel(grad_ref, weight_ref, recv_ref, *rest):
    out_ref = rest[-1]
    for r in range(GROUP):
        out_ref[r] = back_row(weight_ref, grad_ref, r) + recv_ref[r].astype(F32)


def image_back(query, weight_bwd, received, first, step, carried):
    rows, _, columns = query.shape
    block = (GROUP, C_IN, columns)
    operands = [query, weight_bwd, received, *carried]
    in_specs = [
        window(C_OUT, columns, first, step),
        whole(weight_bwd),
        pl.BlockSpec(block, lambda s: (s, 0, 0)),
    ]
    in_specs += [pl.BlockSpec(memory_space=pl.ANY) for _ in carried]
    return pl.pallas_call(
        image_back_kernel,
        grid=(received.shape[0] // GROUP,),
        in_specs=in_specs,
        out_specs=pl.BlockSpec(block, lambda s: ((s * step + first) // GROUP, 0, 0)),
        out_shape=jax.ShapeDtypeStruct((rows - 2, C_IN, columns), F32),
        input_output_aliases={3: 0} if carried else {},
        compiler_params=params(),
        name="image_back",
    )(*operands)


def weight_kernel(query_ref, key_ref, own_ref, partner_ref, out_ref, acc):
    s = pl.program_id(0)
    columns = query_ref.shape[2]
    contract = (((1,), (1,)), ((), ()))

    @pl.when(s == 0)
    def _():
        acc[...] = jnp.zeros_like(acc)

    term = acc[...]
    for r in range(GROUP):
        own = own_ref[r : r + 3].reshape(9 * C_IN, columns)
        partner = partner_ref[r : r + 3].reshape(9 * C_IN, columns)
        term += lax.dot_general(query_ref[r + 1], own, contract, preferred_element_type=F32)
        term += lax.dot_general(key_ref[r + 1], partner, contract, preferred_element_type=F32)
    acc[...] = term

    @pl.when(s == pl.num_programs(0) - 1)
    def _():
        for tap in range(9):
            out_ref[tap] = acc[:, tap * C_IN : (tap + 1) * C_IN].astype(BF16)


def weight_term(query, key, own_taps, partner_taps):
    rows, _, columns = query.shape
    grads = window(C_OUT, columns)
    taps = window(3 * C_IN, columns)
    return pl.pallas_call(
        weight_kernel,
        grid=((rows - 2) // GROUP,),
        in_specs=[grads, grads, taps, taps],
        out_specs=pl.BlockSpec((9, C_OUT, C_IN), lambda s: (0, 0, 0)),
        out_shape=jax.ShapeDtypeStruct((9, C_OUT, C_IN), BF16),
        scratch_shapes=[pltpu.VMEM((C_OUT, 9 * C_IN), F32)],
        compiler_params=params(),
        name="weight_term",
    )(query, key, own_taps, partner_taps)


def passed_along(x, axis, by):
    size = lax.axis_size(axis)
    return lax.ppermute(x, axis, [(i, (i + by) % size) for i in range(size)])


def shifted_bands(x, by):
    size = lax.axis_size("band")
    return lax.ppermute(
        x, "band", [(i, i + by) for i in range(size) if 0 <= i + by < size]
    )


def diagonal(x, by):
    cams, bands = lax.axis_size("cam"), lax.axis_size("band")
    pairs = [
        ((c + 1) % cams * bands + b - by, c * bands + b)
        for c in range(cams)
        for b in range(bands)
        if 0 <= b - by < bands
    ]
    return lax.ppermute(x, ("cam", "band"), pairs)


def lookup(table, position):
    places = jnp.arange(table.shape[0], dtype=jnp.int32)
    return jnp.sum(jnp.where(places == position, table, 0), dtype=jnp.int32)


def summed_everywhere(term):
    axes = ("cam", "band")
    count = lax.axis_size("cam") * lax.axis_size("band")
    pieces = term.reshape(count, -1, C_IN)
    mine = lax.all_to_all(pieces, axes, split_axis=0, concat_axis=0, tiled=True)
    piece = jnp.sum(mine.astype(F32), axis=0, keepdims=True).astype(BF16)
    spread = jnp.broadcast_to(piece, pieces.shape)
    return lax.all_to_all(spread, axes, split_axis=0, concat_axis=0, tiled=True)


def per_device(images, weight, offsets, cotangent):
    image = jnp.transpose(images[0], (1, 0, 2))
    cot = cotangent[0]
    rows = image.shape[0]
    columns = image.shape[2]
    first, last = image[:2], image[-2:]
    low = shifted_bands(jnp.concatenate([last, cot[-1].T[None]], axis=0), 1)
    high = shifted_bands(jnp.concatenate([first, cot[0].T[None]], axis=0), -1)
    inner = passed_along(image[2:-2], "cam", -1)
    edges = passed_along(jnp.concatenate([first, last], axis=0), "cam", -1)
    partner_low = diagonal(last, 1)
    partner_high = diagonal(first, -1)

    offset = lookup(offsets, lax.axis_index("cam")).reshape(1)
    weight_fwd = jnp.transpose(weight, (2, 0, 1, 3)).reshape(C_OUT, 9 * C_IN)
    weight_bwd = jnp.transpose(weight, (1, 3, 0, 2)).reshape(3 * C_IN, 3 * C_OUT)

    total_rows = rows + 2
    own = own_side(
        ((0, rows),), (image,), weight_fwd, cot, total_rows, lambda r: r + 2, lambda r: r + 1, ()
    )
    carried = pair_side(
        offset, ((0, rows - 4),), (inner,), weight_fwd, *own[:3], lambda t: t + 4, ()
    )
    inner_back = key_back(carried[1], weight_bwd, GROUP, GROUP, rows // GROUP - 2)
    sent_inner = passed_along(inner_back, "cam", 1)
    own, carried, low, high = lax.optimization_barrier((own, carried, low, high))
    cot_ends = jnp.stack([low[2].T, cot[0], cot[-1], high[2].T])
    feat, featt, skew, own_taps = own_side(
        ((0, 2), (0, 2), (rows - 2, 2), (0, 2)),
        (low, image, image, high),
        weight_fwd,
        cot_ends,
        total_rows,
        lambda r: jnp.where(r < 2, r, jnp.maximum(r - 4, 0) + rows),
        lambda r: jnp.where(r < 2, r, jnp.maximum(r - 4, 0) + 2),
        own,
    )
    query, key, partner_taps = pair_side(
        offset,
        ((0, 2), (0, 2), (0, 2), (rows - 6, 2), (2, 2), (0, 2)),
        (partner_low, edges, inner, inner, edges, partner_high),
        weight_fwd,
        feat,
        featt,
        skew,
        lambda t: jnp.where(t < 4, t, jnp.maximum(t - 6, 0) + rows - 2),
        carried,
    )
    outer_back = key_back(key, weight_bwd, 0, rows - GROUP, 2)
    sent_outer = passed_along(outer_back, "cam", 1)
    key, sent_inner, _ = lax.optimization_barrier((key, sent_inner, outer_back))
    term = weight_term(query, key, own_taps, partner_taps)
    query, _ = lax.optimization_barrier((query, term))
    image_grad = image_back(query, weight_bwd, sent_inner, GROUP, GROUP, ())
    term, sent_outer, image_grad = lax.optimization_barrier((term, sent_outer, image_grad))
    total = summed_everywhere(term)
    normalizer = 1.0 / math.sqrt(lax.axis_size("cam") * lax.axis_size("band") * rows * columns)
    weight_grad = total.astype(F32).reshape(weight.shape) * normalizer
    query, total = lax.optimization_barrier((query, total))
    image_grad = image_back(query, weight_bwd, sent_outer, 0, rows - GROUP, (image_grad,))
    return (jnp.transpose(image_grad, (1, 0, 2))[None], weight_grad)


def solution(mesh):
    in_specs = (P("cam", None, "band", None), P(), P(), P("cam", "band", None, None))
    out_specs = (P("cam", None, "band", None), P())
    return jax.shard_map(
        per_device, mesh=mesh, in_specs=in_specs, out_specs=out_specs, check_vma=False
    )
```
